32 devices in a mesh: img: 8 (over z, core), txt: 4 (over y, x).
Axes of the slice: x: 2, y: 2, z: 4, core: 2. Of those that a mesh axis runs over, the one named last changes fastest.
Arguments:
- image_emb: float32 [1024, 1536], P('img', 'txt'), may hold values from -0.15625 to 0.15625
- text_emb: float32 [1024, 1536], P('txt', 'img'), may hold values from -0.15625 to 0.15625
- vision_feat: bfloat16 [1024, 5120], P('img', 'txt'), may hold values from -0.125 to 0.125
- positive: int32 [1024], P('img'), may hold values from 0 to 1023, each once
- logit_scale: float32 [1], replicated, may hold values from 5 to 15
- logit_bias: float32 [1], replicated, may hold values from -3 to -1
Outputs:
- grad_image: float32 [1024, 1536], P('img', 'txt')
- grad_text: float32 [1024, 1536], P('txt', 'img')
- grad_proj: float32 [5120, 1536], P('txt', 'img')
The draws below stay inside these ranges and needn't reach their ends.
Inputs may be any that keep to these rules, and one draw needn't show every extreme that they name: `positive`: each text index is the match of exactly one image.
All inputs are finite; a program needn't handle non-finite values.
Results may differ from the reference program's by a relative error of at most 0.0029.
Values may be sent and summed in bfloat16 or wider, within the bound.
A program may use at most 64 MiB of HBM per device.

```python
import jax
import jax.numpy as jnp
from jax import lax

EMB = 1536
VIS = 5120
ROWS_IMG = 128
PAIRS = 1024
N_IMG = 8


def block_levels(key, shape, cuts, low, high):
    def one(dim, parts):
        draws = jax.random.uniform(jax.random.fold_in(jax.random.fold_in(key, 6), dim), (parts,), jnp.float32, low / len(cuts), high / len(cuts))
        return jnp.repeat(jnp.exp(draws), shape[dim] // parts).reshape((-1,) + (1,) * (len(shape) - dim - 1))

    loudness = one(*cuts[0])
    for cut in cuts[1:]:
        loudness = loudness * one(*cut)
    return loudness


def normal_values(rng, extent, deviation, most, cuts=(), kind=jnp.bfloat16):
    values = deviation * jax.random.normal(rng, extent, jnp.float32)
    if cuts:
        values = values * block_levels(rng, extent, cuts, -0.22, 0.18)
    return jnp.clip(values, -most, most).astype(kind)


def setup_inputs(seed: int = 0) -> dict:
    arg_keys = jax.random.split(jax.random.key(seed), 7)
    return {
        "image_emb": normal_values(arg_keys[0], (PAIRS, EMB), (EMB ** -0.5), 0.15625, ((0, 8), (1, 4)), jnp.float32),
        "text_emb": normal_values(arg_keys[1], (PAIRS, EMB), (EMB ** -0.5), 0.15625, ((0, 4), (1, 8)), jnp.float32),
        "vision_feat": normal_values(arg_keys[2], (PAIRS, VIS), 0.02, 0.125, ((0, 8), (1, 4))),
        "positive": jax.random.permutation(arg_keys[3], PAIRS).astype(jnp.int32),
        "logit_scale": jnp.clip(jax.random.uniform(arg_keys[4], (1,), jnp.float32, 5.0, 15.0), 5.0, 15.0),
        "logit_bias": jnp.clip(jax.random.uniform(arg_keys[5], (1,), jnp.float32, -3.0, -1.0), -3.0, -1.0),
    }


def reference(image_emb, text_emb, vision_feat, positive, logit_scale, logit_bias):
    scale = logit_scale[0]
    bias = logit_bias[0]
    blocks = image_emb.reshape(N_IMG, ROWS_IMG, EMB)
    matches = positive.reshape(N_IMG, ROWS_IMG)
    columns = jnp.arange(PAIRS, dtype=jnp.int32)

    def step(carry, item):
        image_block, match_block = item
        logits = scale * jnp.dot(image_block, text_emb.T, precision=lax.Precision.HIGHEST, preferred_element_type=jnp.float32) + bias
        sign = jnp.where(match_block[:, None] == columns[None, :], 1.0, -1.0).astype(jnp.float32)
        slope = -sign * jax.nn.sigmoid(-sign * logits)
        image_grad = scale * jnp.dot(slope, text_emb, precision=lax.Precision.HIGHEST, preferred_element_type=jnp.float32)
        carry = carry + scale * jnp.dot(slope.T, image_block, precision=lax.Precision.HIGHEST, preferred_element_type=jnp.float32)
        return carry, image_grad

    start = jnp.zeros((PAIRS, EMB), jnp.float32)
    grad_text, pieces = lax.scan(step, start, (blocks, matches))
    grad_image = pieces.reshape(PAIRS, EMB)
    image_low = grad_image.astype(jnp.bfloat16)
    grad_proj = jnp.dot(vision_feat.T, image_low, preferred_element_type=jnp.float32)
    return grad_image, grad_text, grad_proj
```

```python
import functools

import jax
import jax.numpy as jnp
from jax import lax
from jax.experimental import pallas as pl
from jax.experimental.pallas import tpu as pltpu
from jax.sharding import PartitionSpec as P

MESH = pl.DeviceIdType.MESH
F32 = jnp.float32
BF16 = jnp.bfloat16


def kernel(
    n_img, n_txt,
    scale_ref, bias_ref, pos_ref, img_ref, txt_ref, vis_ref,
    gi_ref, gt_ref, gp_ref,
    img_full, txt_full, vis_full, pimg, rs_img, gsend, grecv, low_send, low_recv,
    ptxt, txt_pair, txt_low, rs_txt,
    i_s, i_r, t_s, t_r, tp_s, tp_r, v_s, v_r, vp_s, vp_r, a_s, a_r, g_s, g_r,
    l_s, l_r, m_s, m_r, x_s, x_r, r_s, r_r,
):
    pairs = n_img // 2
    me_i = lax.axis_index("img")
    me_t = lax.axis_index("txt")
    p = me_i // 2
    c = lax.rem(me_i, 2)
    mate = 2 * p + 1 - c
    et = img_ref.shape[0]
    ei = txt_ref.shape[0]
    rows = img_ref.shape[1]
    cols = txt_ref.shape[1]
    part = rows // n_txt

    def img_of(k):
        return lax.rem(me_i + k, n_img)

    def txt_of(k):
        return lax.rem(me_t + k, n_txt)

    def pair_of(k):
        return lax.rem(p + k + pairs, pairs)

    def remote(src, dst, ss, rs, i, t):
        return pltpu.make_async_remote_copy(
            src_ref=src, dst_ref=dst, send_sem=ss, recv_sem=rs,
            device_id=(i, t), device_id_type=MESH,
        )

    def txt_rows(i):
        return pl.ds(pl.multiple_of(i * ei, ei), ei)

    def img_rows(t):
        return pl.ds(pl.multiple_of(t * et, et), et)

    def vis_rows(i):
        return pl.ds(pl.multiple_of(i * rows, rows), rows)

    barrier = pltpu.get_barrier_semaphore()
    for k in range(1, n_img):
        pl.semaphore_signal(barrier, inc=1, device_id=(img_of(k), me_t), device_id_type=MESH)
    for k in range(1, n_txt):
        pl.semaphore_signal(barrier, inc=1, device_id=(me_i, txt_of(k)), device_id_type=MESH)
    pl.semaphore_wait(barrier, n_img + n_txt - 2)

    mine_t = txt_full.at[txt_rows(me_i), :]
    text_z = [
        remote(txt_ref, mine_t, t_s.at[k - 1], t_r.at[k - 1], 2 * pair_of(k) + c, me_t)
        for k in range(1, pairs)
    ]
    text_mate = [remote(txt_ref, mine_t, tp_s.at[0], tp_r.at[0], mate, me_t)]
    image_x = [
        remote(img_ref, img_full.at[img_rows(me_t), :], i_s.at[k - 1], i_r.at[k - 1], me_i, txt_of(k))
        for k in range(1, n_txt)
    ]
    for copy in text_z + text_mate + image_x:
        copy.start()
    vis_ring = []
    vis_mate = []

    def send_vis(step):
        block = vis_rows(2 * pair_of(-step) + c)
        src = vis_ref if step == 0 else vis_full.at[block, :]
        if step < pairs - 1:
            ring = remote(src, vis_full.at[block, :], v_s.at[step], v_r.at[step], 2 * pair_of(1) + c, me_t)
            ring.start()
            vis_ring.append(ring)
        pair = remote(src, vis_full.at[block, :], vp_s.at[step], vp_r.at[step], mate, me_t)
        pair.start()
        vis_mate.append(pair)

    send_vis(0)
    txt_full[txt_rows(me_i), :] = txt_ref[...]
    img_full[img_rows(me_t), :] = img_ref[...]
    vis_full[vis_rows(me_i), :] = vis_ref[...]
    for k in range(1, pairs):
        text_z[k - 1].wait_recv()
        block = txt_full.at[txt_rows(2 * pair_of(-k) + c), :]
        copy = remote(block, block, tp_s.at[k], tp_r.at[k], mate, me_t)
        copy.start()
        text_mate.append(copy)
    for copy in image_x + text_mate:
        copy.wait_recv()

    scale = scale_ref[0]
    bias = bias_ref[0]
    image = img_full[...]
    text = txt_full[...]
    logits = scale * lax.dot_general(
        image, text, (((0,), (0,)), ((), ())), preferred_element_type=F32
    ) + bias
    column = me_t * cols + lax.broadcasted_iota(jnp.int32, (rows, cols), 1)
    sign = jnp.where(pos_ref[...] == column, 1.0, -1.0).astype(F32)
    slope = -sign / (1.0 + jnp.exp(sign * logits))
    high = slope.astype(BF16)
    rest = (slope - high.astype(F32)).astype(BF16)

    nt = (((1,), (1,)), ((), ()))
    pimg[...] = lax.dot_general(high, text, nt, preferred_element_type=F32) + lax.dot_general(
        rest, text, nt, preferred_element_type=F32
    )

    def part_rows(t):
        return pl.ds(pl.multiple_of(t * part, part), part)

    image_rs = [
        remote(pimg.at[part_rows(txt_of(k)), :], rs_img.at[k - 1], a_s.at[k - 1], a_r.at[k - 1], me_i, txt_of(k))
        for k in range(1, n_txt)
    ]
    for copy in image_rs:
        copy.start()

    ptxt[...] = jnp.dot(image, high, preferred_element_type=F32) + jnp.dot(
        image, rest, preferred_element_type=F32
    )
    text_pair = [
        remote(ptxt.at[txt_rows(2 * q + 1 - c), :], txt_pair.at[q], x_s.at[q], x_r.at[q], mate, me_t)
        for q in range(pairs)
    ]
    for copy in text_pair:
        copy.start()

    def step_vis(step):
        vis_ring[step - 1].wait_recv()
        send_vis(step)

    for step in range(1, pairs - 1):
        step_vis(step)

    for copy in image_rs:
        copy.wait_recv()
    total = pimg[part_rows(me_t), :]
    for k in range(n_txt - 1):
        total = total + rs_img[k]
    total = scale * total
    low = total.astype(BF16)
    for i in range(n_img):
        low_send[i] = low[:, i * ei:(i + 1) * ei]
    low_z = [
        remote(low_send.at[img_of(k)], low_recv.at[me_i, me_t], l_s.at[k - 1], l_r.at[k - 1], img_of(k), me_t)
        for k in range(1, n_img)
    ]
    for copy in low_z:
        copy.start()
    for t in range(n_txt):
        gsend[t] = total[:, t * et:(t + 1) * et]
    grad_x = [
        remote(gsend.at[txt_of(k)], grecv.at[me_t], g_s.at[k - 1], g_r.at[k - 1], me_i, txt_of(k))
        for k in range(1, n_txt)
    ]
    low_recv[me_i, me_t] = low_send[me_i]
    for copy in low_z:
        copy.wait_recv()
    low_x = [
        remote(low_recv.at[:, me_t], low_recv.at[:, me_t], m_s.at[k - 1], m_r.at[k - 1], me_i, txt_of(k))
        for k in range(1, n_txt)
    ]
    for copy in low_x + grad_x:
        copy.start()

    step_vis(pairs - 1)

    for q in range(pairs):
        text_pair[q].wait_recv()
        txt_pair[q] = txt_pair[q] + ptxt[txt_rows(2 * q + c), :]
        txt_low[q] = txt_pair[q].astype(BF16)
    text_rs = [
        remote(txt_low.at[pair_of(k)], rs_txt.at[k - 1], r_s.at[k - 1], r_r.at[k - 1], 2 * pair_of(k) + c, me_t)
        for k in range(1, pairs)
    ]
    for copy in text_rs:
        copy.start()

    for copy in low_x + vis_mate:
        copy.wait_recv()
    if part % 16:
        low_all = low_recv[...].astype(F32).reshape(n_img * rows, ei).astype(BF16)
    else:
        low_all = low_recv[...].reshape(n_img * rows, ei)
    gp_ref[...] = lax.dot_general(
        low_all, vis_full[...], (((0,), (0,)), ((), ())), preferred_element_type=F32
    )

    for copy in grad_x:
        copy.wait_recv()
    gi_ref[...] = grecv[...]
    gi_ref[me_t] = gsend[me_t]
    for copy in text_rs:
        copy.wait_recv()
    total = txt_pair[p]
    for k in range(pairs - 1):
        total = total + rs_txt[k].astype(F32)
    gt_ref[...] = scale * total
    for copy in text_z + text_mate + image_x + vis_ring + vis_mate + image_rs + text_pair + low_z + low_x + grad_x + text_rs:
        copy.wait_send()


def per_device(n_img, n_txt, image_emb, text_emb, vision_feat, positive, logit_scale, logit_bias):
    image = image_emb.T.astype(BF16)
    text = text_emb.T.astype(BF16)
    et, rows = image.shape
    ei, cols = text.shape
    emb = et * n_txt
    vis = vision_feat.shape[1]
    part = rows // n_txt
    pairs = n_img // 2
    dma = lambda n: pltpu.SemaphoreType.DMA((n,))
    vmem = pl.BlockSpec(memory_space=pltpu.VMEM)
    smem = pl.BlockSpec(memory_space=pltpu.SMEM)
    gi, gt, gp = pl.pallas_call(
        functools.partial(kernel, n_img, n_txt),
        out_shape=(
            jax.ShapeDtypeStruct((n_txt, part, et), F32),
            jax.ShapeDtypeStruct((ei, cols), F32),
            jax.ShapeDtypeStruct((ei, vis), F32),
        ),
        in_specs=[smem, smem, vmem, vmem, vmem, vmem],
        out_specs=(vmem, vmem, vmem),
        scratch_shapes=[
            pltpu.VMEM((emb, rows), BF16),
            pltpu.VMEM((emb, cols), BF16),
            pltpu.VMEM((n_img * rows, vis), BF16),
            pltpu.VMEM((rows, emb), F32),
            pltpu.VMEM((n_txt - 1, part, emb), F32),
            pltpu.VMEM((n_txt, part, et), F32),
            pltpu.VMEM((n_txt, part, et), F32),
            pltpu.VMEM((n_img, part, ei), BF16),
            pltpu.VMEM((n_img, n_txt, part, ei), BF16),
            pltpu.VMEM((emb, cols), F32),
            pltpu.VMEM((pairs, ei, cols), F32),
            pltpu.VMEM((pairs, ei, cols), BF16),
            pltpu.VMEM((pairs - 1, ei, cols), BF16),
            dma(n_txt - 1), dma(n_txt - 1),
            dma(pairs - 1), dma(pairs - 1), dma(pairs), dma(pairs),
            dma(pairs - 1), dma(pairs - 1), dma(pairs), dma(pairs),
            dma(n_txt - 1), dma(n_txt - 1), dma(n_txt - 1), dma(n_txt - 1),
            dma(n_img - 1), dma(n_img - 1), dma(n_txt - 1), dma(n_txt - 1),
            dma(pairs), dma(pairs), dma(pairs - 1), dma(pairs - 1),
        ],
        compiler_params=pltpu.CompilerParams(
            collective_id=0, has_side_effects=True, vmem_limit_bytes=60 * 1024 * 1024
        ),
    )(logit_scale, logit_bias, positive.reshape(rows, 1), image, text, vision_feat)
    return gi.reshape(rows, et), gt.T, gp.T


def solution(mesh):
    placed = (P("img", "txt"), P("txt", "img"), P("img", "txt"), P("img"), P(), P())
    return jax.shard_map(
        functools.partial(per_device, mesh.shape["img"], mesh.shape["txt"]),
        mesh=mesh,
        in_specs=placed,
        out_specs=(P("img", "txt"), P("txt", "img"), P("txt", "img")),
        check_vma=False,
    )
```

```python
import functools

import jax
import jax.numpy as jnp
from jax import lax
from jax.experimental import pallas as pl
from jax.experimental.pallas import tpu as pltpu
from jax.sharding import PartitionSpec as P

MESH = pl.DeviceIdType.MESH
F32 = jnp.float32
BF16 = jnp.bfloat16


def kernel(
    n_img, n_txt,
    scale_ref, bias_ref, pos_ref, img_ref, txt_ref, vis_ref,
    gi_ref, gt_ref, gp_ref,
    img_full, txt_full, txt_rest, vis_full, pimg, rs_img, gsend, grecv, low_send, low_recv,
    ptxt, txt_pair, txt_low, rs_txt,
    i_s, i_r, t_s, t_r, tp_s, tp_r, tl_s, tl_r, v_s, v_r, w_s, w_r, vp_s, vp_r, a_s, a_r, g_s, g_r,
    l_s, l_r, m_s, m_r, x_s, x_r, r_s, r_r,
):
    pairs = n_img // 2
    me_i = lax.axis_index("img")
    me_t = lax.axis_index("txt")
    p = me_i // 2
    c = lax.rem(me_i, 2)
    mate = 2 * p + 1 - c
    rows, et = img_ref.shape
    cols, ei = txt_ref.shape
    part = rows // n_txt

    def img_of(k):
        return lax.rem(me_i + k, n_img)

    def txt_of(k):
        return lax.rem(me_t + k, n_txt)

    def pair_of(k):
        return lax.rem(p + k + pairs, pairs)

    def remote(src, dst, ss, rs, i, t):
        return pltpu.make_async_remote_copy(
            src_ref=src, dst_ref=dst, send_sem=ss, recv_sem=rs,
            device_id=(i, t), device_id_type=MESH,
        )

    def txt_rows(i):
        return pl.ds(pl.multiple_of(i * ei, ei), ei)

    def img_rows(t):
        return pl.ds(pl.multiple_of(t * et, et), et)

    def vis_rows(i):
        return pl.ds(pl.multiple_of(i * rows, rows), rows)

    txt_rest[...] = jnp.zeros_like(txt_rest)
    barrier = pltpu.get_barrier_semaphore()
    for k in range(1, n_img):
        pl.semaphore_signal(barrier, inc=1, device_id=(img_of(k), me_t), device_id_type=MESH)
    for k in range(1, n_txt):
        pl.semaphore_signal(barrier, inc=1, device_id=(me_i, txt_of(k)), device_id_type=MESH)
    text_own = txt_ref[...].T
    text_high = text_own.astype(BF16)
    txt_full[txt_rows(me_i), :] = text_high
    img_full[img_rows(me_t), :] = img_ref[...].T.astype(BF16)
    pl.semaphore_wait(barrier, n_img + n_txt - 2)
    txt_rest[txt_rows(me_i), :] = (text_own - text_high.astype(F32)).astype(BF16)

    mine_t = txt_full.at[txt_rows(me_i), :]
    mine_x = img_full.at[img_rows(me_t), :]
    mine_rest = txt_rest.at[txt_rows(me_i), :]
    text_z = [
        remote(mine_t, mine_t, t_s.at[k - 1], t_r.at[k - 1], 2 * pair_of(k) + c, me_t)
        for k in range(1, pairs)
    ]
    text_mate = [remote(mine_t, mine_t, tp_s.at[0], tp_r.at[0], mate, me_t)]
    rest_mate = remote(mine_rest, mine_rest, tl_s.at[0], tl_r.at[0], mate, me_t)
    image_x = [
        remote(mine_x, mine_x, i_s.at[k - 1], i_r.at[k - 1], me_i, txt_of(k))
        for k in range(1, n_txt)
    ]
    for copy in text_z + image_x + text_mate + [rest_mate]:
        copy.start()
    vis_mate = []

    def up_copy(step):
        block = vis_full.at[vis_rows(2 * pair_of(-step) + c), :]
        return remote(vis_ref if step == 0 else block, block, v_s.at[step], v_r.at[step], 2 * pair_of(1) + c, me_t)

    def down_copy(step):
        block = vis_full.at[vis_rows(2 * pair_of(step) + c), :]
        return remote(vis_ref if step == 0 else block, block, w_s.at[step], w_r.at[step], 2 * pair_of(-1) + c, me_t)

    def up_sends(step):
        return jnp.logical_and(p - step >= 0, p < pairs - 1)

    def down_sends(step):
        return jnp.logical_and(p + step < pairs, p > 0)

    def mate_copy(block, src, slot):
        return remote(src, block, vp_s.at[slot], vp_r.at[slot], mate, me_t)

    def send_vis(step):
        if step == 0:
            block = vis_full.at[vis_rows(me_i), :]
            mate_copy(block, vis_ref, 0).start()
        else:
            @pl.when(p - step >= 0)
            def _():
                up_copy(step - 1).wait_recv()
                block = vis_full.at[vis_rows(2 * pair_of(-step) + c), :]
                mate_copy(block, block, step).start()

            @pl.when(p + step < pairs)
            def _():
                down_copy(step - 1).wait_recv()
                block = vis_full.at[vis_rows(2 * pair_of(step) + c), :]
                mate_copy(block, block, pairs - 1 + step).start()

        if step < pairs - 1:
            @pl.when(up_sends(step))
            def _():
                up_copy(step).start()

            @pl.when(down_sends(step))
            def _():
                down_copy(step).start()

    vis_full[vis_rows(me_i), :] = vis_ref[...]
    for k in range(1, pairs):
        text_z[k - 1].wait_recv()
        block = txt_full.at[txt_rows(2 * pair_of(-k) + c), :]
        copy = remote(block, block, tp_s.at[k], tp_r.at[k], mate, me_t)
        copy.start()
        text_mate.append(copy)
    send_vis(0)
    for copy in image_x + text_mate:
        copy.wait_recv()

    scale = scale_ref[0]
    bias = bias_ref[0]
    image = img_full[...]
    text = txt_full[...]
    logits = scale * lax.dot_general(
        image, text, (((0,), (0,)), ((), ())), preferred_element_type=F32
    ) + bias
    column = me_t * cols + lax.broadcasted_iota(jnp.int32, (rows, cols), 1)
    match = jnp.broadcast_to(pos_ref[...].astype(F32), (cols, rows)).T.astype(jnp.int32)
    sign = jnp.where(match == column, 1.0, -1.0).astype(F32)
    slope = -sign / (1.0 + jnp.exp(sign * logits))
    high = slope.astype(BF16)
    rest = (slope - high.astype(F32)).astype(BF16)

    nt = (((1,), (1,)), ((), ()))
    rest_mate.wait_recv()
    pimg[...] = (
        lax.dot_general(high, text, nt, preferred_element_type=F32)
        + lax.dot_general(rest, text, nt, preferred_element_type=F32)
        + lax.dot_general(high, txt_rest[...], nt, preferred_element_type=F32)
    )

    def part_rows(t):
        return pl.ds(pl.multiple_of(t * part, part), part)

    image_rs = [
        remote(pimg.at[part_rows(txt_of(k)), :], rs_img.at[k - 1], a_s.at[k - 1], a_r.at[k - 1], me_i, txt_of(k))
        for k in range(1, n_txt)
    ]
    for copy in image_rs:
        copy.start()

    ptxt[...] = jnp.dot(image, high, preferred_element_type=F32) + jnp.dot(
        image, rest, preferred_element_type=F32
    )
    text_pair = [
        remote(ptxt.at[txt_rows(2 * q + 1 - c), :], txt_pair.at[q], x_s.at[q], x_r.at[q], mate, me_t)
        for q in range(pairs)
    ]
    for copy in text_pair:
        copy.start()

    for step in range(1, pairs - 1):
        send_vis(step)

    for copy in image_rs:
        copy.wait_recv()
    total = pimg[part_rows(me_t), :]
    for k in range(n_txt - 1):
        total = total + rs_img[k]
    total = scale * total
    low = total.astype(BF16)
    for i in range(n_img):
        low_send[i] = low[:, i * ei:(i + 1) * ei]
    low_z = [
        remote(low_send.at[img_of(k)], low_recv.at[me_i, me_t], l_s.at[k - 1], l_r.at[k - 1], img_of(k), me_t)
        for k in range(1, n_img)
    ]
    for copy in low_z:
        copy.start()
    for t in range(n_txt):
        gsend[t] = total[:, t * et:(t + 1) * et]
    grad_x = [
        remote(gsend.at[txt_of(k)], grecv.at[me_t], g_s.at[k - 1], g_r.at[k - 1], me_i, txt_of(k))
        for k in range(1, n_txt)
    ]
    low_recv[me_i, me_t] = low_send[me_i]
    send_vis(pairs - 1)
    for copy in low_z:
        copy.wait_recv()
    low_x = [
        remote(low_recv.at[:, me_t], low_recv.at[:, me_t], m_s.at[k - 1], m_r.at[k - 1], me_i, txt_of(k))
        for k in range(1, n_txt)
    ]
    for copy in low_x + grad_x:
        copy.start()

    for q in range(pairs):
        text_pair[q].wait_recv()
        txt_pair[q] = txt_pair[q] + ptxt[txt_rows(2 * q + c), :]
        txt_low[q] = txt_pair[q].astype(BF16)
    text_rs = [
        remote(txt_low.at[pair_of(k)], rs_txt.at[k - 1], r_s.at[k - 1], r_r.at[k - 1], 2 * pair_of(k) + c, me_t)
        for k in range(1, pairs)
    ]
    for copy in text_rs:
        copy.start()

    for copy in low_x:
        copy.wait_recv()
    mate_copy(vis_full.at[vis_rows(mate), :], vis_ref, 0).wait_recv()
    for step in range(1, pairs):
        @pl.when(p - step >= 0)
        def _():
            mate_copy(vis_full.at[vis_rows(mate), :], vis_ref, step).wait_recv()

        @pl.when(p + step < pairs)
        def _():
            mate_copy(vis_full.at[vis_rows(mate), :], vis_ref, pairs - 1 + step).wait_recv()
    if part % 16:
        low_all = low_recv[...].astype(F32).reshape(n_img * rows, ei).astype(BF16)
    else:
        low_all = low_recv[...].reshape(n_img * rows, ei)
    gp_ref[...] = lax.dot_general(
        low_all, vis_full[...], (((0,), (0,)), ((), ())), preferred_element_type=F32
    ).T

    for copy in grad_x:
        copy.wait_recv()
    gi_ref[...] = grecv[...]
    gi_ref[me_t] = gsend[me_t]
    for copy in text_rs:
        copy.wait_recv()
    total = txt_pair[p]
    for k in range(pairs - 1):
        total = total + rs_txt[k].astype(F32)
    gt_ref[...] = (scale * total).T
    for copy in text_z + text_mate + [rest_mate] + image_x + image_rs + text_pair + low_z + low_x + grad_x + text_rs:
        copy.wait_send()
    mate_copy(vis_full.at[vis_rows(mate), :], vis_ref, 0).wait_send()
    for step in range(pairs):
        if step > 0:
            @pl.when(p - step >= 0)
            def _():
                mate_copy(vis_full.at[vis_rows(mate), :], vis_ref, step).wait_send()

            @pl.when(p + step < pairs)
            def _():
                mate_copy(vis_full.at[vis_rows(mate), :], vis_ref, pairs - 1 + step).wait_send()

        if step < pairs - 1:
            @pl.when(up_sends(step))
            def _():
                up_copy(step).wait_send()

            @pl.when(down_sends(step))
            def _():
                down_copy(step).wait_send()


def per_device(n_img, n_txt, image_emb, text_emb, vision_feat, positive, logit_scale, logit_bias):
    rows, et = image_emb.shape
    cols, ei = text_emb.shape
    emb = et * n_txt
    vis = vision_feat.shape[1]
    part = rows // n_txt
    pairs = n_img // 2
    dma = lambda n: pltpu.SemaphoreType.DMA((n,))
    vmem = pl.BlockSpec(memory_space=pltpu.VMEM)
    smem = pl.BlockSpec(memory_space=pltpu.SMEM)
    gi, gt, gp = pl.pallas_call(
        functools.partial(kernel, n_img, n_txt),
        out_shape=(
            jax.ShapeDtypeStruct((n_txt, part, et), F32),
            jax.ShapeDtypeStruct((cols, ei), F32),
            jax.ShapeDtypeStruct((vis, ei), F32),
        ),
        in_specs=[smem, smem, vmem, vmem, vmem, vmem],
        out_specs=(vmem, vmem, vmem),
        scratch_shapes=[
            pltpu.VMEM((emb, rows), BF16),
            pltpu.VMEM((emb, cols), BF16),
            pltpu.VMEM((emb, cols), BF16),
            pltpu.VMEM((n_img * rows, vis), BF16),
            pltpu.VMEM((rows, emb), F32),
            pltpu.VMEM((n_txt - 1, part, emb), F32),
            pltpu.VMEM((n_txt, part, et), F32),
            pltpu.VMEM((n_txt, part, et), F32),
            pltpu.VMEM((n_img, part, ei), BF16),
            pltpu.VMEM((n_img, n_txt, part, ei), BF16),
            pltpu.VMEM((emb, cols), F32),
            pltpu.VMEM((pairs, ei, cols), F32),
            pltpu.VMEM((pairs, ei, cols), BF16),
            pltpu.VMEM((pairs - 1, ei, cols), BF16),
            dma(n_txt - 1), dma(n_txt - 1),
            dma(pairs - 1), dma(pairs - 1), dma(pairs), dma(pairs), dma(1), dma(1),
            dma(pairs - 1), dma(pairs - 1), dma(pairs - 1), dma(pairs - 1), dma(2 * pairs - 1), dma(2 * pairs - 1),
            dma(n_txt - 1), dma(n_txt - 1), dma(n_txt - 1), dma(n_txt - 1),
            dma(n_img - 1), dma(n_img - 1), dma(n_txt - 1), dma(n_txt - 1),
            dma(pairs), dma(pairs), dma(pairs - 1), dma(pairs - 1),
        ],
        compiler_params=pltpu.CompilerParams(
            collective_id=0, has_side_effects=True, vmem_limit_bytes=60 * 1024 * 1024
        ),
    )(logit_scale, logit_bias, positive.reshape(1, rows), image_emb, text_emb, vision_feat)
    return gi.reshape(rows, et), gt, gp


def solution(mesh):
    placed = (P("img", "txt"), P("txt", "img"), P("img", "txt"), P("img"), P(), P())
    return jax.shard_map(
        functools.partial(per_device, mesh.shape["img"], mesh.shape["txt"]),
        mesh=mesh,
        in_specs=placed,
        out_specs=(P("img", "txt"), P("txt", "img"), P("txt", "img")),
        check_vma=False,
    )
```

```python
import functools

import jax
import jax.numpy as jnp
from jax import lax
from jax.experimental import pallas as pl
from jax.experimental.pallas import tpu as pltpu
from jax.sharding import PartitionSpec as P

MESH = pl.DeviceIdType.MESH
PIECES = 2
F32 = jnp.float32
BF16 = jnp.bfloat16


def kernel(
    n_img, n_txt,
    scale_ref, bias_ref, pos_ref, img_ref, txt_ref, vis_ref,
    gi_ref, gt_ref, gp_ref,
    img_full, txt_full, txt_rest, vis_full, pimg, rs_img, gsend, grecv, low_send, low_recv,
    ptxt, txt_pair, txt_low, rs_txt,
    i_s, i_r, t_s, t_r, tp_s, tp_r, tl_s, tl_r, v_s, v_r, w_s, w_r, vp_s, vp_r, a_s, a_r, g_s, g_r,
    l_s, l_r, m_s, m_r, x_s, x_r, r_s, r_r,
):
    pairs = n_img // 2
    me_i = lax.axis_index("img")
    me_t = lax.axis_index("txt")
    p = me_i // 2
    c = lax.rem(me_i, 2)
    mate = 2 * p + 1 - c
    rows, et = img_ref.shape
    ei, cols = txt_ref.shape
    part = rows // n_txt
    piece = rows // PIECES

    def img_of(k):
        return lax.rem(me_i + k, n_img)

    def txt_of(k):
        return lax.rem(me_t + k, n_txt)

    def pair_of(k):
        return lax.rem(p + k + pairs, pairs)

    def remote(src, dst, ss, rs, i, t):
        return pltpu.make_async_remote_copy(
            src_ref=src, dst_ref=dst, send_sem=ss, recv_sem=rs,
            device_id=(i, t), device_id_type=MESH,
        )

    def txt_rows(i):
        return pl.ds(pl.multiple_of(i * ei, ei), ei)

    def img_rows(t):
        return pl.ds(pl.multiple_of(t * et, et), et)

    def vis_rows(i, h):
        return pl.ds(pl.multiple_of(i * rows + h * piece, piece), piece)

    txt_rest[...] = jnp.zeros_like(txt_rest)
    barrier = pltpu.get_barrier_semaphore()
    for k in range(1, n_img):
        pl.semaphore_signal(barrier, inc=1, device_id=(img_of(k), me_t), device_id_type=MESH)
    for k in range(1, n_txt):
        pl.semaphore_signal(barrier, inc=1, device_id=(me_i, txt_of(k)), device_id_type=MESH)
    text_own = txt_ref[...]
    text_high = text_own.astype(BF16)
    txt_full[txt_rows(me_i), :] = text_high
    img_full[img_rows(me_t), :] = img_ref[...].T.astype(BF16)
    pl.semaphore_wait(barrier, n_img + n_txt - 2)
    txt_rest[txt_rows(me_i), :] = (text_own - text_high.astype(F32)).astype(BF16)

    mine_t = txt_full.at[txt_rows(me_i), :]
    mine_x = img_full.at[img_rows(me_t), :]
    mine_rest = txt_rest.at[txt_rows(me_i), :]
    text_z = [
        remote(mine_t, mine_t, t_s.at[k - 1], t_r.at[k - 1], 2 * pair_of(k) + c, me_t)
        for k in range(1, pairs)
    ]
    text_mate = [remote(mine_t, mine_t, tp_s.at[0], tp_r.at[0], mate, me_t)]
    rest_mate = remote(mine_rest, mine_rest, tl_s.at[0], tl_r.at[0], mate, me_t)
    image_x = [
        remote(mine_x, mine_x, i_s.at[k - 1], i_r.at[k - 1], me_i, txt_of(k))
        for k in range(1, n_txt)
    ]
    for copy in text_z + image_x + text_mate + [rest_mate]:
        copy.start()
    vis_mate = []

    def up_copy(step, h):
        block = vis_full.at[vis_rows(2 * pair_of(-step) + c, h), :]
        n = step * PIECES + h
        return remote(vis_own(h) if step == 0 else block, block, v_s.at[n], v_r.at[n], 2 * pair_of(1) + c, me_t)

    def down_copy(step, h):
        block = vis_full.at[vis_rows(2 * pair_of(step) + c, h), :]
        n = step * PIECES + h
        return remote(vis_own(h) if step == 0 else block, block, w_s.at[n], w_r.at[n], 2 * pair_of(-1) + c, me_t)

    def vis_own(h):
        return vis_ref.at[pl.ds(h * piece, piece), :]

    def up_sends(step):
        return jnp.logical_and(p - step >= 0, p < pairs - 1)

    def down_sends(step):
        return jnp.logical_and(p + step < pairs, p > 0)

    def mate_copy(offset, h):
        block = vis_full.at[vis_rows(2 * pair_of(-offset) + c, h), :]
        n = (offset if offset >= 0 else pairs - 1 - offset) * PIECES + h
        return remote(vis_own(h) if offset == 0 else block, block, vp_s.at[n], vp_r.at[n], mate, me_t)

    def send_vis(step, h):
        if step == 0:
            mate_copy(0, h).start()
        else:
            @pl.when(p - step >= 0)
            def _():
                up_copy(step - 1, h).wait_recv()

            @pl.when(p + step < pairs)
            def _():
                down_copy(step - 1, h).wait_recv()

        if step < pairs - 1:
            @pl.when(up_sends(step))
            def _():
                up_copy(step, h).start()

            @pl.when(down_sends(step))
            def _():
                down_copy(step, h).start()

        if step > 0:
            @pl.when(p - step >= 0)
            def _():
                mate_copy(step, h).start()

            @pl.when(p + step < pairs)
            def _():
                mate_copy(-step, h).start()

    for h in range(PIECES):
        send_vis(0, h)
    vis_full[pl.ds(pl.multiple_of(me_i * rows, rows), rows), :] = vis_ref[...]
    for k in range(1, pairs):
        text_z[k - 1].wait_recv()
        block = txt_full.at[txt_rows(2 * pair_of(-k) + c), :]
        copy = remote(block, block, tp_s.at[k], tp_r.at[k], mate, me_t)
        copy.start()
        text_mate.append(copy)
    for copy in image_x + text_mate:
        copy.wait_recv()

    scale = scale_ref[0]
    bias = bias_ref[0]
    image = img_full[...]
    text = txt_full[...]
    logits = scale * lax.dot_general(
        image, text, (((0,), (0,)), ((), ())), preferred_element_type=F32
    ) + bias
    column = me_t * cols + lax.broadcasted_iota(jnp.int32, (rows, cols), 1)
    match = jnp.broadcast_to(pos_ref[...].astype(F32), (cols, rows)).T.astype(jnp.int32)
    sign = jnp.where(match == column, 1.0, -1.0).astype(F32)
    slope = -sign / (1.0 + jnp.exp(sign * logits))
    high = slope.astype(BF16)
    rest = (slope - high.astype(F32)).astype(BF16)

    nt = (((1,), (1,)), ((), ()))
    rest_mate.wait_recv()
    pimg[...] = (
        lax.dot_general(high, text, nt, preferred_element_type=F32)
        + lax.dot_general(rest, text, nt, preferred_element_type=F32)
        + lax.dot_general(high, txt_rest[...], nt, preferred_element_type=F32)
    )

    def part_rows(t):
        return pl.ds(pl.multiple_of(t * part, part), part)

    image_rs = [
        remote(pimg.at[part_rows(txt_of(k)), :], rs_img.at[k - 1], a_s.at[k - 1], a_r.at[k - 1], me_i, txt_of(k))
        for k in range(1, n_txt)
    ]
    for copy in image_rs:
        copy.start()

    ptxt[...] = jnp.dot(image, high, preferred_element_type=F32) + jnp.dot(
        image, rest, preferred_element_type=F32
    )
    text_pair = [
        remote(ptxt.at[txt_rows(2 * q + 1 - c), :], txt_pair.at[q], x_s.at[q], x_r.at[q], mate, me_t)
        for q in range(pairs)
    ]
    for copy in text_pair:
        copy.start()

    for step in range(1, pairs - 1):
        for h in range(PIECES):
            send_vis(step, h)

    for copy in image_rs:
        copy.wait_recv()
    total = pimg[part_rows(me_t), :]
    for k in range(n_txt - 1):
        total = total + rs_img[k]
    total = scale * total
    low = total.astype(BF16)
    for i in range(n_img):
        low_send[i] = low[:, i * ei:(i + 1) * ei]
    low_z = [
        remote(low_send.at[img_of(k)], low_recv.at[me_i, me_t], l_s.at[k - 1], l_r.at[k - 1], img_of(k), me_t)
        for k in range(1, n_img)
    ]
    for copy in low_z:
        copy.start()
    for t in range(n_txt):
        gsend[t] = total[:, t * et:(t + 1) * et]
    grad_x = [
        remote(gsend.at[txt_of(k)], grecv.at[me_t], g_s.at[k - 1], g_r.at[k - 1], me_i, txt_of(k))
        for k in range(1, n_txt)
    ]
    low_recv[me_i, me_t] = low_send[me_i]
    for copy in low_z:
        copy.wait_recv()
    low_x = [
        remote(low_recv.at[:, me_t], low_recv.at[:, me_t], m_s.at[k - 1], m_r.at[k - 1], me_i, txt_of(k))
        for k in range(1, n_txt)
    ]
    for copy in low_x + grad_x:
        copy.start()

    for h in range(PIECES):
        send_vis(pairs - 1, h)

    for q in range(pairs):
        text_pair[q].wait_recv()
        txt_pair[q] = txt_pair[q] + ptxt[txt_rows(2 * q + c), :]
        txt_low[q] = txt_pair[q].astype(BF16)
    text_rs = [
        remote(txt_low.at[pair_of(k)], rs_txt.at[k - 1], r_s.at[k - 1], r_r.at[k - 1], 2 * pair_of(k) + c, me_t)
        for k in range(1, pairs)
    ]
    for copy in text_rs:
        copy.start()

    for copy in low_x:
        copy.wait_recv()
    for h in range(PIECES):
        mate_copy(0, h).wait_recv()
        for step in range(1, pairs):
            @pl.when(p - step >= 0)
            def _():
                mate_copy(step, h).wait_recv()

            @pl.when(p + step < pairs)
            def _():
                mate_copy(-step, h).wait_recv()
    if part % 16:
        low_all = low_recv[...].astype(F32).reshape(n_img * rows, ei).astype(BF16)
    else:
        low_all = low_recv[...].reshape(n_img * rows, ei)
    gp_ref[...] = lax.dot_general(
        low_all, vis_full[...], (((0,), (0,)), ((), ())), preferred_element_type=F32
    )

    for copy in grad_x:
        copy.wait_recv()
    gi_ref[...] = grecv[...]
    gi_ref[me_t] = gsend[me_t]
    for copy in text_rs:
        copy.wait_recv()
    total = txt_pair[p]
    for k in range(pairs - 1):
        total = total + rs_txt[k].astype(F32)
    gt_ref[...] = scale * total
    for copy in text_z + text_mate + [rest_mate] + image_x + image_rs + text_pair + low_z + low_x + grad_x + text_rs:
        copy.wait_send()
    for h in range(PIECES):
        mate_copy(0, h).wait_send()
        for step in range(pairs):
            if step > 0:
                @pl.when(p - step >= 0)
                def _():
                    mate_copy(step, h).wait_send()

                @pl.when(p + step < pairs)
                def _():
                    mate_copy(-step, h).wait_send()

            if step < pairs - 1:
                @pl.when(up_sends(step))
                def _():
                    up_copy(step, h).wait_send()

                @pl.when(down_sends(step))
                def _():
                    down_copy(step, h).wait_send()


def per_device(n_img, n_txt, image_emb, text_emb, vision_feat, positive, logit_scale, logit_bias):
    rows, et = image_emb.shape
    cols, ei = text_emb.shape
    emb = et * n_txt
    vis = vision_feat.shape[1]
    part = rows // n_txt
    pairs = n_img // 2
    dma = lambda n: pltpu.SemaphoreType.DMA((n,))
    vmem = pl.BlockSpec(memory_space=pltpu.VMEM)
    smem = pl.BlockSpec(memory_space=pltpu.SMEM)
    gi, gt, gp = pl.pallas_call(
        functools.partial(kernel, n_img, n_txt),
        out_shape=(
            jax.ShapeDtypeStruct((n_txt, part, et), F32),
            jax.ShapeDtypeStruct((ei, cols), F32),
            jax.ShapeDtypeStruct((ei, vis), F32),
        ),
        in_specs=[smem, smem, vmem, vmem, vmem, vmem],
        out_specs=(vmem, vmem, vmem),
        scratch_shapes=[
            pltpu.VMEM((emb, rows), BF16),
            pltpu.VMEM((emb, cols), BF16),
            pltpu.VMEM((emb, cols), BF16),
            pltpu.VMEM((n_img * rows, vis), BF16),
            pltpu.VMEM((rows, emb), F32),
            pltpu.VMEM((n_txt - 1, part, emb), F32),
            pltpu.VMEM((n_txt, part, et), F32),
            pltpu.VMEM((n_txt, part, et), F32),
            pltpu.VMEM((n_img, part, ei), BF16),
            pltpu.VMEM((n_img, n_txt, part, ei), BF16),
            pltpu.VMEM((emb, cols), F32),
            pltpu.VMEM((pairs, ei, cols), F32),
            pltpu.VMEM((pairs, ei, cols), BF16),
            pltpu.VMEM((pairs - 1, ei, cols), BF16),
            dma(n_txt - 1), dma(n_txt - 1),
            dma(pairs - 1), dma(pairs - 1), dma(pairs), dma(pairs), dma(1), dma(1),
            *[dma(PIECES * (pairs - 1))] * 4, *[dma(PIECES * (2 * pairs - 1))] * 2,
            dma(n_txt - 1), dma(n_txt - 1), dma(n_txt - 1), dma(n_txt - 1),
            dma(n_img - 1), dma(n_img - 1), dma(n_txt - 1), dma(n_txt - 1),
            dma(pairs), dma(pairs), dma(pairs - 1), dma(pairs - 1),
        ],
        compiler_params=pltpu.CompilerParams(
            collective_id=0, has_side_effects=True, vmem_limit_bytes=60 * 1024 * 1024
        ),
    )(logit_scale, logit_bias, positive.reshape(1, rows), image_emb, text_emb.T, vision_feat)
    return gi.reshape(rows, et), gt.T, gp.T


def solution(mesh):
    placed = (P("img", "txt"), P("txt", "img"), P("img", "txt"), P("img"), P(), P())
    return jax.shard_map(
        functools.partial(per_device, mesh.shape["img"], mesh.shape["txt"]),
        mesh=mesh,
        in_specs=placed,
        out_specs=(P("img", "txt"), P("txt", "img"), P("txt", "img")),
        check_vma=False,
    )
```

```python
import functools

import jax
import jax.numpy as jnp
from jax import lax
from jax.experimental import pallas as pl
from jax.experimental.pallas import tpu as pltpu
from jax.sharding import PartitionSpec as P

MESH = pl.DeviceIdType.MESH
PIECES = 4
F32 = jnp.float32
BF16 = jnp.bfloat16


def kernel(
    n_img, n_txt,
    scale_ref, bias_ref, pos_ref, img_ref, txt_ref, vis_ref,
    gi_ref, gt_ref, gp_ref,
    img_full, txt_full, txt_rest, vis_full, pimg, rs_img, gsend, grecv, low_send, low_recv,
    ptxt, txt_pair, txt_low, rs_txt,
    i_s, i_r, t_s, t_r, tp_s, tp_r, tl_s, tl_r, v_s, v_r, w_s, w_r, vp_s, vp_r, a_s, a_r, g_s, g_r,
    l_s, l_r, m_s, m_r, x_s, x_r, r_s, r_r,
):
    pairs = n_img // 2
    me_i = lax.axis_index("img")
    me_t = lax.axis_index("txt")
    p = me_i // 2
    c = lax.rem(me_i, 2)
    mate = 2 * p + 1 - c
    rows, et = img_ref.shape
    ei, cols = txt_ref.shape
    part = rows // n_txt
    piece = rows // PIECES

    def img_of(k):
        return lax.rem(me_i + k, n_img)

    def txt_of(k):
        return lax.rem(me_t + k, n_txt)

    def pair_of(k):
        return lax.rem(p + k + pairs, pairs)

    def remote(src, dst, ss, rs, i, t):
        return pltpu.make_async_remote_copy(
            src_ref=src, dst_ref=dst, send_sem=ss, recv_sem=rs,
            device_id=(i, t), device_id_type=MESH,
        )

    def txt_rows(i):
        return pl.ds(pl.multiple_of(i * ei, ei), ei)

    def img_rows(t):
        return pl.ds(pl.multiple_of(t * et, et), et)

    def vis_rows(i, h):
        return pl.ds(pl.multiple_of(i * rows + h * piece, piece), piece)

    txt_rest[...] = jnp.zeros_like(txt_rest)
    barrier = pltpu.get_barrier_semaphore()
    for k in range(1, n_img):
        pl.semaphore_signal(barrier, inc=1, device_id=(img_of(k), me_t), device_id_type=MESH)
    for k in range(1, n_txt):
        pl.semaphore_signal(barrier, inc=1, device_id=(me_i, txt_of(k)), device_id_type=MESH)
    text_own = txt_ref[...]
    text_high = text_own.astype(BF16)
    txt_full[txt_rows(me_i), :] = text_high
    img_full[img_rows(me_t), :] = img_ref[...].T.astype(BF16)
    pl.semaphore_wait(barrier, n_img + n_txt - 2)
    txt_rest[txt_rows(me_i), :] = (text_own - text_high.astype(F32)).astype(BF16)

    mine_t = txt_full.at[txt_rows(me_i), :]
    mine_x = img_full.at[img_rows(me_t), :]
    mine_rest = txt_rest.at[txt_rows(me_i), :]
    text_z = [
        remote(mine_t, mine_t, t_s.at[k - 1], t_r.at[k - 1], 2 * pair_of(k) + c, me_t)
        for k in range(1, pairs)
    ]
    text_mate = [remote(mine_t, mine_t, tp_s.at[0], tp_r.at[0], mate, me_t)]
    rest_mate = remote(mine_rest, mine_rest, tl_s.at[0], tl_r.at[0], mate, me_t)
    image_x = [
        remote(mine_x, mine_x, i_s.at[k - 1], i_r.at[k - 1], me_i, txt_of(k))
        for k in range(1, n_txt)
    ]
    for copy in text_z + image_x + text_mate + [rest_mate]:
        copy.start()
    vis_mate = []

    def up_copy(step, h):
        block = vis_full.at[vis_rows(2 * pair_of(-step) + c, h), :]
        n = step * PIECES + h
        return remote(vis_own(h) if step == 0 else block, block, v_s.at[n], v_r.at[n], 2 * pair_of(1) + c, me_t)

    def down_copy(step, h):
        block = vis_full.at[vis_rows(2 * pair_of(step) + c, h), :]
        n = step * PIECES + h
        return remote(vis_own(h) if step == 0 else block, block, w_s.at[n], w_r.at[n], 2 * pair_of(-1) + c, me_t)

    def vis_own(h):
        return vis_ref.at[pl.ds(h * piece, piece), :]

    def up_sends(step):
        return jnp.logical_and(p - step >= 0, p < pairs - 1)

    def down_sends(step):
        return jnp.logical_and(p + step < pairs, p > 0)

    def mate_copy(offset, h):
        block = vis_full.at[vis_rows(2 * pair_of(-offset) + c, h), :]
        n = (offset if offset >= 0 else pairs - 1 - offset) * PIECES + h
        return remote(vis_own(h) if offset == 0 else block, block, vp_s.at[n], vp_r.at[n], mate, me_t)

    def send_vis(step, h):
        if step == 0:
            mate_copy(0, h).start()
        else:
            @pl.when(p - step >= 0)
            def _():
                up_copy(step - 1, h).wait_recv()

            @pl.when(p + step < pairs)
            def _():
                down_copy(step - 1, h).wait_recv()

        if step < pairs - 1:
            @pl.when(up_sends(step))
            def _():
                up_copy(step, h).start()

            @pl.when(down_sends(step))
            def _():
                down_copy(step, h).start()

        if step > 0:
            @pl.when(p - step >= 0)
            def _():
                mate_copy(step, h).start()

            @pl.when(p + step < pairs)
            def _():
                mate_copy(-step, h).start()

    for h in range(PIECES):
        send_vis(0, h)
    vis_full[pl.ds(pl.multiple_of(me_i * rows, rows), rows), :] = vis_ref[...]
    for k in range(1, pairs):
        text_z[k - 1].wait_recv()
        block = txt_full.at[txt_rows(2 * pair_of(-k) + c), :]
        copy = remote(block, block, tp_s.at[k], tp_r.at[k], mate, me_t)
        copy.start()
        text_mate.append(copy)
    for copy in image_x + text_mate:
        copy.wait_recv()

    scale = scale_ref[0]
    bias = bias_ref[0]
    image = img_full[...]
    text = txt_full[...]
    logits = scale * lax.dot_general(
        image, text, (((0,), (0,)), ((), ())), preferred_element_type=F32
    ) + bias
    column = me_t * cols + lax.broadcasted_iota(jnp.int32, (rows, cols), 1)
    match = jnp.broadcast_to(pos_ref[...].astype(F32), (cols, rows)).T.astype(jnp.int32)
    sign = jnp.where(match == column, 1.0, -1.0).astype(F32)
    slope = -sign / (1.0 + jnp.exp(sign * logits))
    high = slope.astype(BF16)
    rest = (slope - high.astype(F32)).astype(BF16)

    nt = (((1,), (1,)), ((), ()))
    rest_mate.wait_recv()
    pimg[...] = (
        lax.dot_general(high, text, nt, preferred_element_type=F32)
        + lax.dot_general(rest, text, nt, preferred_element_type=F32)
        + lax.dot_general(high, txt_rest[...], nt, preferred_element_type=F32)
    )

    def part_rows(t):
        return pl.ds(pl.multiple_of(t * part, part), part)

    image_rs = [
        remote(pimg.at[part_rows(txt_of(k)), :], rs_img.at[k - 1], a_s.at[k - 1], a_r.at[k - 1], me_i, txt_of(k))
        for k in range(1, n_txt)
    ]
    for copy in image_rs:
        copy.start()

    for step in range(1, pairs - 1):
        for h in range(PIECES):
            send_vis(step, h)
    ptxt[...] = jnp.dot(image, high, preferred_element_type=F32) + jnp.dot(
        image, rest, preferred_element_type=F32
    )
    text_pair = [
        remote(ptxt.at[txt_rows(2 * q + 1 - c), :], txt_pair.at[q], x_s.at[q], x_r.at[q], mate, me_t)
        for q in range(pairs)
    ]
    for copy in text_pair:
        copy.start()


    for copy in image_rs:
        copy.wait_recv()
    total = pimg[part_rows(me_t), :]
    for k in range(n_txt - 1):
        total = total + rs_img[k]
    total = scale * total
    low = total.astype(BF16)
    for i in range(n_img):
        low_send[i] = low[:, i * ei:(i + 1) * ei]
    low_z = [
        remote(low_send.at[img_of(k)], low_recv.at[me_i, me_t], l_s.at[k - 1], l_r.at[k - 1], img_of(k), me_t)
        for k in range(1, n_img)
    ]
    for copy in low_z:
        copy.start()
    for t in range(n_txt):
        gsend[t] = total[:, t * et:(t + 1) * et]
    grad_x = [
        remote(gsend.at[txt_of(k)], grecv.at[me_t], g_s.at[k - 1], g_r.at[k - 1], me_i, txt_of(k))
        for k in range(1, n_txt)
    ]
    low_recv[me_i, me_t] = low_send[me_i]
    for copy in low_z:
        copy.wait_recv()
    low_x = [
        remote(low_recv.at[:, me_t], low_recv.at[:, me_t], m_s.at[k - 1], m_r.at[k - 1], me_i, txt_of(k))
        for k in range(1, n_txt)
    ]
    for copy in low_x + grad_x:
        copy.start()

    for h in range(PIECES):
        send_vis(pairs - 1, h)

    for q in range(pairs):
        text_pair[q].wait_recv()
        txt_pair[q] = txt_pair[q] + ptxt[txt_rows(2 * q + c), :]
        txt_low[q] = txt_pair[q].astype(BF16)
    text_rs = [
        remote(txt_low.at[pair_of(k)], rs_txt.at[k - 1], r_s.at[k - 1], r_r.at[k - 1], 2 * pair_of(k) + c, me_t)
        for k in range(1, pairs)
    ]
    for copy in text_rs:
        copy.start()

    for copy in low_x:
        copy.wait_recv()
    for h in range(PIECES):
        mate_copy(0, h).wait_recv()
        for step in range(1, pairs):
            @pl.when(p - step >= 0)
            def _():
                mate_copy(step, h).wait_recv()

            @pl.when(p + step < pairs)
            def _():
                mate_copy(-step, h).wait_recv()
    if part % 16:
        low_all = low_recv[...].astype(F32).reshape(n_img * rows, ei).astype(BF16)
    else:
        low_all = low_recv[...].reshape(n_img * rows, ei)
    gp_ref[...] = lax.dot_general(
        low_all, vis_full[...], (((0,), (0,)), ((), ())), preferred_element_type=F32
    )

    for copy in grad_x:
        copy.wait_recv()
    gi_ref[...] = grecv[...]
    gi_ref[me_t] = gsend[me_t]
    for copy in text_rs:
        copy.wait_recv()
    total = txt_pair[p]
    for k in range(pairs - 1):
        total = total + rs_txt[k].astype(F32)
    gt_ref[...] = scale * total
    for copy in text_z + text_mate + [rest_mate] + image_x + image_rs + text_pair + low_z + low_x + grad_x + text_rs:
        copy.wait_send()
    for h in range(PIECES):
        mate_copy(0, h).wait_send()
        for step in range(pairs):
            if step > 0:
                @pl.when(p - step >= 0)
                def _():
                    mate_copy(step, h).wait_send()

                @pl.when(p + step < pairs)
                def _():
                    mate_copy(-step, h).wait_send()

            if step < pairs - 1:
                @pl.when(up_sends(step))
                def _():
                    up_copy(step, h).wait_send()

                @pl.when(down_sends(step))
                def _():
                    down_copy(step, h).wait_send()


def per_device(n_img, n_txt, image_emb, text_emb, vision_feat, positive, logit_scale, logit_bias):
    rows, et = image_emb.shape
    cols, ei = text_emb.shape
    emb = et * n_txt
    vis = vision_feat.shape[1]
    part = rows // n_txt
    pairs = n_img // 2
    dma = lambda n: pltpu.SemaphoreType.DMA((n,))
    vmem = pl.BlockSpec(memory_space=pltpu.VMEM)
    smem = pl.BlockSpec(memory_space=pltpu.SMEM)
    gi, gt, gp = pl.pallas_call(
        functools.partial(kernel, n_img, n_txt),
        out_shape=(
            jax.ShapeDtypeStruct((n_txt, part, et), F32),
            jax.ShapeDtypeStruct((ei, cols), F32),
            jax.ShapeDtypeStruct((ei, vis), F32),
        ),
        in_specs=[smem, smem, vmem, vmem, vmem, vmem],
        out_specs=(vmem, vmem, vmem),
        scratch_shapes=[
            pltpu.VMEM((emb, rows), BF16),
            pltpu.VMEM((emb, cols), BF16),
            pltpu.VMEM((emb, cols), BF16),
            pltpu.VMEM((n_img * rows, vis), BF16),
            pltpu.VMEM((rows, emb), F32),
            pltpu.VMEM((n_txt - 1, part, emb), F32),
            pltpu.VMEM((n_txt, part, et), F32),
            pltpu.VMEM((n_txt, part, et), F32),
            pltpu.VMEM((n_img, part, ei), BF16),
            pltpu.VMEM((n_img, n_txt, part, ei), BF16),
            pltpu.VMEM((emb, cols), F32),
            pltpu.VMEM((pairs, ei, cols), F32),
            pltpu.VMEM((pairs, ei, cols), BF16),
            pltpu.VMEM((pairs - 1, ei, cols), BF16),
            dma(n_txt - 1), dma(n_txt - 1),
            dma(pairs - 1), dma(pairs - 1), dma(pairs), dma(pairs), dma(1), dma(1),
            *[dma(PIECES * (pairs - 1))] * 4, *[dma(PIECES * (2 * pairs - 1))] * 2,
            dma(n_txt - 1), dma(n_txt - 1), dma(n_txt - 1), dma(n_txt - 1),
            dma(n_img - 1), dma(n_img - 1), dma(n_txt - 1), dma(n_txt - 1),
            dma(pairs), dma(pairs), dma(pairs - 1), dma(pairs - 1),
        ],
        compiler_params=pltpu.CompilerParams(
            collective_id=0, has_side_effects=True, vmem_limit_bytes=60 * 1024 * 1024
        ),
    )(logit_scale, logit_bias, positive.reshape(1, rows), image_emb, text_emb.T, vision_feat)
    return gi.reshape(rows, et), gt.T, gp.T


def solution(mesh):
    placed = (P("img", "txt"), P("txt", "img"), P("img", "txt"), P("img"), P(), P())
    return jax.shard_map(
        functools.partial(per_device, mesh.shape["img"], mesh.shape["txt"]),
        mesh=mesh,
        in_specs=placed,
        out_specs=(P("img", "txt"), P("txt", "img"), P("txt", "img")),
        check_vma=False,
    )
```
